32 devices in a mesh: seq: 8 (over z, y), tp: 4 (over x, core).
Axes of the slice: x: 2, y: 2, z: 4, core: 2. Of those that a mesh axis runs over, the one named last changes fastest.
Arguments:
- prefill_tokens: bfloat16 [4096, 2304], P('seq'), may hold values from -6 to 6
- decode_tokens: bfloat16 [64, 2304], P('seq'), may hold values from -6 to 6
- attention_gain: float32 [2304], replicated, may hold values from 0.5 to 1.5
- qkv_weight: bfloat16 [2304, 3, 2304], P(None, None, 'tp'), may hold values from -0.125 to 0.125
- out_weight: bfloat16 [2304, 2304], P('tp'), may hold values from -0.375 to 0.375
- feedforward_gain: float32 [2304], replicated, may hold values from 0.5 to 1.5
- prefill_cache: bfloat16 [8, 2, 1024, 2304], P('seq', None, None, 'tp'), may hold values from -420 to 420
- prefill_offsets: int32 [8], P('seq'), may hold values from 0 to 1024, as said below
- decode_cache: bfloat16 [64, 2, 256, 2304], P('seq', None, None, 'tp'), may hold values from -420 to 420
- decode_lengths: int32 [64], P('seq'), may hold values from 1 to 256, as said below
- request_slot: int32 [64], replicated, may hold values from 0 to 63, each once
Outputs:
- prefill_hidden: bfloat16 [4096, 2304], P('seq')
- decode_hidden: bfloat16 [64, 2304], P('seq')
- prefill_normed: bfloat16 [4096, 2304], P('seq')
- decode_normed: bfloat16 [64, 2304], P('seq')
The draws below stay inside these ranges and needn't reach their ends.
Inputs may be any that keep to these rules, and one draw needn't show every extreme that they name: `request_slot`: each slot is named by exactly one request. `decode_lengths`: some slot holds exactly 256 positions. `prefill_offsets`: some request has exactly 1024 cached positions.
All inputs are finite; a program needn't handle non-finite values.
Results may differ from the reference program's by a relative error of at most 0.014.
The reference program's roundings to bfloat16 on the way (of `normed_in`, `projected`, `weights` and `attended`) count: a program that leaves them out, or rounds other values in their place, can miss the bound.
Values may be sent and summed in bfloat16 or wider, within the bound.
A program may use at most 128 MiB of HBM per device.

```python
import math
import jax
import jax.numpy as jnp
from jax import lax

D = 2304
HEADS = 36
HEAD = 64
SPAN = 512
CMAX = 256
PMAX = 1024
NDEC = 64
PRE_ROWS = 4096
N_SEQ = 8
N_TP = 4


def kv_values(key, shape):
    return jax.random.truncated_normal(key, -6.0, 6.0, shape, jnp.float32)


def draw_decode_cache(key, part):
    return kv_values(key, (NDEC, 2, CMAX, HEADS * HEAD)).astype(jnp.bfloat16)


def draw_prefill_cache(key, part):
    return kv_values(key, (N_SEQ, 2, PMAX, HEADS * HEAD)).astype(jnp.bfloat16)


def draw_decode_lengths(key, part):
    lengths = jax.random.randint(key, (NDEC,), 1, CMAX + 1, dtype=jnp.int32)
    longest = jax.random.randint(jax.random.fold_in(key, 7), (), 0, NDEC, dtype=jnp.int32)
    return lengths.at[longest].set(CMAX)


def draw_prefill_offsets(key, part):
    offsets = jax.random.randint(key, (N_SEQ,), 0, PMAX + 1, dtype=jnp.int32)
    longest = jax.random.randint(jax.random.fold_in(key, 11), (), 0, N_SEQ, dtype=jnp.int32)
    return offsets.at[longest].set(PMAX)


def levels(rng, dims, shards, low, high):
    level, own = 1.0, jax.random.fold_in(rng, 6)
    for dim, shards_of in shards:
        draws = jnp.exp(jax.random.uniform(jax.random.fold_in(own, dim), (shards_of,), jnp.float32, low / len(shards), high / len(shards)))
        level = level * jnp.repeat(draws, dims[dim] // shards_of).reshape([-1 if axis == dim else 1 for axis in range(len(dims))])
    return level


def bell_draw(own_key, shape, deviation, reach, cuts=(), kind=jnp.bfloat16):
    array = jax.random.normal(own_key, shape, jnp.float32) * deviation
    if len(cuts) > 0:
        array = levels(own_key, shape, cuts, -0.22, 0.18) * array
    return jnp.clip(array, min=-reach, max=reach).astype(kind)


def setup_inputs(seed: int = 0) -> dict:
    keys = jax.random.split(jax.random.key(seed), 12)
    prefill_tokens = bell_draw(keys[0], (PRE_ROWS, D), 1.0, 6.0, ((0, 8),))
    decode_tokens = bell_draw(keys[1], (NDEC, D), 1.0, 6.0, ((0, 8),))
    attention_gain = jnp.clip(1.0 + 0.1 * jax.random.normal(keys[2], (D,), jnp.float32), 0.5, 1.5)
    qkv_weight = bell_draw(keys[3], (D, 3, HEADS * HEAD), D ** -0.5, 0.125, ((2, 4),))
    out_weight = bell_draw(keys[4], (HEADS * HEAD, D), (4 * HEAD) ** -0.5, 0.375, ((0, 4),))
    feedforward_gain = jnp.clip(1.0 + 0.1 * jax.random.normal(keys[5], (D,), jnp.float32), 0.5, 1.5)
    prefill_cache = draw_prefill_cache(jax.random.fold_in(keys[11], 71), 0)
    prefill_offsets = draw_prefill_offsets(jax.random.fold_in(keys[11], 71), 0)
    decode_cache = draw_decode_cache(jax.random.fold_in(keys[11], 71), 0)
    decode_lengths = draw_decode_lengths(jax.random.fold_in(keys[11], 71), 0)
    request_slot = jax.random.permutation(keys[10], NDEC).astype(jnp.int32)
    return {"prefill_tokens": prefill_tokens, "decode_tokens": decode_tokens, "attention_gain": attention_gain, "qkv_weight": qkv_weight, "out_weight": out_weight, "feedforward_gain": feedforward_gain, "prefill_cache": prefill_cache, "prefill_offsets": prefill_offsets, "decode_cache": decode_cache, "decode_lengths": decode_lengths, "request_slot": request_slot}


RMS_EPSILON = 1e-05
ROPE_BASE = 10000.0
NEGATIVE = -1e+30

def rms_norm(stream, gain):
    widened = stream.astype(jnp.float32)
    inverse = lax.rsqrt(lax.optimization_barrier(jnp.mean(widened * widened, axis=-1, keepdims=True)) + RMS_EPSILON)
    return widened * inverse * gain

def rotate(vectors, positions):
    half_dim = vectors.shape[-1] // 2
    exponent = jnp.arange(half_dim, dtype=jnp.float32) * (2.0 / vectors.shape[-1])
    frequency = ROPE_BASE ** (-exponent)
    angles = positions[:, None] * frequency[None, :]
    cosine = jnp.cos(angles)[:, None, :]
    sine_part = jnp.sin(angles)[:, None, :]
    first_half = vectors[..., :half_dim]
    second_half = vectors[..., half_dim:]
    return jnp.concatenate([first_half * cosine - second_half * sine_part, second_half * cosine + first_half * sine_part], axis=-1)

def softmax_mix(scores, visible, values_all):
    scores = jnp.where(visible, scores, NEGATIVE)
    row_peak = lax.optimization_barrier(jnp.max(scores, axis=-1, keepdims=True))
    exps = jnp.exp(scores - row_peak)
    weights = (exps / lax.optimization_barrier(jnp.sum(exps, axis=-1, keepdims=True))).astype(jnp.bfloat16)
    return jnp.einsum('hqk,khe->qhe', weights.astype(jnp.float32), values_all.astype(jnp.float32))

def reference(prefill_tokens, decode_tokens, attention_gain, qkv_weight, out_weight, feedforward_gain, prefill_cache, prefill_offsets, decode_cache, decode_lengths, request_slot):
    score_scale = 1.0 / math.sqrt(HEAD)
    tokens_all = jnp.concatenate([prefill_tokens, decode_tokens], axis=0)
    normed_in = rms_norm(tokens_all, attention_gain).astype(jnp.bfloat16)
    projected = jnp.dot(normed_in, qkv_weight.reshape(D, 3 * HEADS * HEAD), preferred_element_type=jnp.float32).astype(jnp.bfloat16)
    projected = projected.reshape(-1, 3, HEADS, HEAD)
    prefill_part = projected[:N_SEQ * SPAN].reshape(N_SEQ, SPAN, 3, HEADS, HEAD)
    decode_part = projected[N_SEQ * SPAN:]

    def prefill_one(inputs):
        block_rows, cache_pair, offset = inputs
        positions = offset.astype(jnp.float32) + jnp.arange(SPAN, dtype=jnp.float32)
        queries = rotate(block_rows[:, 0].astype(jnp.float32), positions).astype(jnp.bfloat16)
        new_keys = rotate(block_rows[:, 1].astype(jnp.float32), positions).astype(jnp.bfloat16)
        keys_all = jnp.concatenate([cache_pair[0].reshape(PMAX, HEADS, HEAD), new_keys], axis=0)
        values_all = jnp.concatenate([cache_pair[1].reshape(PMAX, HEADS, HEAD), block_rows[:, 2]], axis=0)
        scores = jnp.einsum('qhe,khe->hqk', queries.astype(jnp.float32), keys_all.astype(jnp.float32)) * score_scale
        cache_visible = jnp.arange(PMAX, dtype=jnp.int32) < offset
        causal = jnp.arange(SPAN, dtype=jnp.int32)[None, :] <= jnp.arange(SPAN, dtype=jnp.int32)[:, None]
        visible = jnp.concatenate([jnp.broadcast_to(cache_visible[None, :], (SPAN, PMAX)), causal], axis=1)
        attended = softmax_mix(scores, visible[None], values_all)
        return attended.reshape(SPAN, HEADS * HEAD).astype(jnp.bfloat16)
    prefill_out = lax.map(prefill_one, (prefill_part, prefill_cache, prefill_offsets)).reshape(N_SEQ * SPAN, HEADS * HEAD)

    def decode_one(inputs):
        block_rows, slot_index = inputs
        cache_pair = decode_cache[slot_index]
        length = decode_lengths[slot_index]
        positions = length.astype(jnp.float32).reshape(1)
        queries = rotate(block_rows[None, 0].astype(jnp.float32), positions).astype(jnp.bfloat16)
        new_keys = rotate(block_rows[None, 1].astype(jnp.float32), positions).astype(jnp.bfloat16)
        keys_all = jnp.concatenate([cache_pair[0].reshape(CMAX, HEADS, HEAD), new_keys], axis=0)
        values_all = jnp.concatenate([cache_pair[1].reshape(CMAX, HEADS, HEAD), block_rows[None, 2]], axis=0)
        scores = jnp.einsum('qhe,khe->hqk', queries.astype(jnp.float32), keys_all.astype(jnp.float32)) * score_scale
        visible = jnp.concatenate([jnp.arange(CMAX, dtype=jnp.int32) < length, jnp.ones((1,), dtype=bool)])
        attended = softmax_mix(scores, visible[None, None, :], values_all)
        return attended.reshape(HEADS * HEAD).astype(jnp.bfloat16)
    decode_out = lax.map(decode_one, (decode_part, request_slot))
    attended_all = jnp.concatenate([prefill_out, decode_out], axis=0)
    group_width = HEADS * HEAD // N_TP
    combined = jnp.zeros((attended_all.shape[0], D), jnp.float32)
    for group_index in range(N_TP):
        low = group_index * group_width
        partial_value = jnp.dot(attended_all[:, low:low + group_width], out_weight[low:low + group_width], preferred_element_type=jnp.float32).astype(jnp.bfloat16)
        partial_value = lax.optimization_barrier(partial_value)
        combined = combined + partial_value.astype(jnp.float32)
    hidden = (tokens_all.astype(jnp.float32) + combined).astype(jnp.bfloat16)
    normed = rms_norm(hidden, feedforward_gain).astype(jnp.bfloat16)
    split_row = N_SEQ * SPAN
    return (hidden[:split_row], hidden[split_row:], normed[:split_row], normed[split_row:])
```

```python
import functools

import jax
import jax.numpy as jnp
from jax import lax
from jax.experimental import pallas as pl
from jax.experimental.pallas import tpu as pltpu
from jax.sharding import PartitionSpec as P

HEAD = 64
HALF = HEAD // 2
RMS_EPSILON = 1e-05
ROPE_BASE = 10000.0
NEGATIVE = -1e30
MIB = 1 << 20
F32, BF16 = jnp.float32, jnp.bfloat16
MESH = pl.DeviceIdType.MESH
VMEM = pltpu.VMEM
VSPEC = pl.BlockSpec(memory_space=pltpu.VMEM)
ASPEC = pl.BlockSpec(memory_space=pl.ANY)


def dot(a, b, ca, cb):
    return lax.dot_general(a, b, (((ca,), (cb,)), ((), ())), preferred_element_type=F32)


def rms_rows(x, gain):
    inverse = lax.rsqrt(jnp.mean(x * x, axis=-1, keepdims=True) + RMS_EPSILON)
    return (x * inverse * gain).astype(BF16)


def rotate_columns(x, cosine, sine, scale):
    pieces = []
    for head in range(x.shape[0] // HEAD):
        a = x[head * HEAD : head * HEAD + HALF]
        b = x[head * HEAD + HALF : (head + 1) * HEAD]
        pieces.append(a * cosine - b * sine)
        pieces.append(b * cosine + a * sine)
    turned = jnp.concatenate(pieces, axis=0).astype(BF16)
    return turned if scale is None else (turned.astype(F32) * scale).astype(BF16)


def project_kernel(tok_ref, dtok_ref, gain_ref, w_ref, cos_ref, sin_ref, out_ref, dec_ref, normed, dnormed):
    part = pl.program_id(0)
    rows = tok_ref.shape[0]

    @pl.when(part == 0)
    def _():
        @pl.loop(0, rows // 64)
        def _(i):
            span = pl.ds(pl.multiple_of(i * 64, 64), 64)
            normed[span, :] = rms_rows(tok_ref[span, :].astype(F32), gain_ref[...])

        dnormed[...] = rms_rows(dtok_ref[...].astype(F32), gain_ref[...])

    w = w_ref[0]
    product = dot(w, normed[...], 1, 1).astype(BF16)
    dec_ref[0] = dot(dnormed[...], w, 1, 1).astype(BF16)

    @pl.when(part == 2)
    def _():
        out_ref[0] = product

    @pl.when(part < 2)
    def _():
        scale = jnp.where(part == 0, 0.125, 1.0)
        out_ref[0] = rotate_columns(product.astype(F32), cos_ref[...], sin_ref[...], scale)


def project(tokens, decode_tokens, gain, w, cosine, sine):
    rows, width = tokens.shape
    drows = decode_tokens.shape[0]
    local = w.shape[1]
    whole = lambda shape: pl.BlockSpec(shape, lambda i: (0,) * len(shape), pipeline_mode=pl.Buffered(1))
    return pl.pallas_call(
        project_kernel,
        grid=(3,),
        in_specs=[
            whole((rows, width)),
            whole((drows, width)),
            whole((1, width)),
            pl.BlockSpec((1, local, width), lambda i: (i, 0, 0)),
            whole((HALF, rows)),
            whole((HALF, rows)),
        ],
        out_specs=[
            pl.BlockSpec((1, local, rows), lambda i: (i, 0, 0)),
            pl.BlockSpec((1, drows, local), lambda i: (i, 0, 0)),
        ],
        out_shape=[
            jax.ShapeDtypeStruct((3, local, rows), BF16),
            jax.ShapeDtypeStruct((3, drows, local), BF16),
        ],
        scratch_shapes=[VMEM((rows, width), BF16), VMEM((drows, width), BF16)],
        compiler_params=pltpu.CompilerParams(vmem_limit_bytes=40 * MIB),
        name="project",
    )(tokens, decode_tokens, gain, w, cosine, sine)


def decode_kernel(
    n, dec_ref, pick_ref, back_ref, cos_ref, sin_ref, bias_ref, cache_hbm, out_ref,
    arrived, results, cache, cache_sem, send1, recv1, send2, recv2,
):
    slots = dec_ref.shape[1]
    local = dec_ref.shape[2]
    heads = local // HEAD
    rows = 16
    me = lax.axis_index("seq")
    load = pltpu.make_async_copy(cache_hbm, cache, cache_sem)
    load.start()

    barrier = pltpu.get_barrier_semaphore()
    for step in range(1, n):
        pl.semaphore_signal(barrier, inc=1, device_id={"seq": lax.rem(me + step, n)}, device_id_type=MESH)
    pl.semaphore_wait(barrier, n - 1)

    def exchange(buffer, send, recv):
        copies = [
            pltpu.make_async_remote_copy(
                src_ref=buffer.at[me],
                dst_ref=buffer.at[me],
                send_sem=send.at[step],
                recv_sem=recv.at[step],
                device_id={"seq": lax.rem(me + step, n)},
                device_id_type=MESH,
            )
            for step in range(1, n)
        ]
        for copy in copies:
            copy.start()
        for copy in copies:
            copy.wait()

    arrived[me] = dec_ref[...]
    exchange(arrived, send1, recv1)

    def gathered(part):
        return arrived[:, part].astype(F32).reshape(n * slots, local).astype(BF16)

    pick = pick_ref[...]
    q = rotate_columns(dot(gathered(0), pick, 0, 1).astype(BF16).astype(F32), cos_ref[...], sin_ref[...], 0.125).astype(F32)
    k = rotate_columns(dot(gathered(1), pick, 0, 1).astype(BF16).astype(F32), cos_ref[...], sin_ref[...], None).astype(F32)
    v = dot(pick, gathered(2), 1, 0).astype(BF16).astype(F32)
    load.wait()

    own_head = (
        lax.broadcasted_iota(jnp.int32, (local, rows), 0) // HEAD
        == lax.broadcasted_iota(jnp.int32, (local, rows), 1)
    )
    own_lane = (
        lax.broadcasted_iota(jnp.int32, (rows, local), 1) // HEAD
        == lax.broadcasted_iota(jnp.int32, (rows, local), 0)
    )
    attended = []
    for s in range(slots):
        query = jnp.where(own_head, q[:, s : s + 1], 0.0).astype(BF16)
        key = jnp.broadcast_to(k[:, s : s + 1], (local, 128)).astype(BF16)
        scores = dot(query, cache[s, 0], 0, 0) + bias_ref[s]
        own = dot(query, key, 0, 0)[:, :1]
        peak = jnp.maximum(jnp.max(scores, axis=-1, keepdims=True), own)
        exps = jnp.exp(scores - peak)
        own_exp = jnp.exp(own - peak)
        total = jnp.sum(exps, axis=-1, keepdims=True) + own_exp
        weights = (exps / total).astype(BF16)
        own_weight = (own_exp / total).astype(BF16).astype(F32)
        mixed = dot(weights, cache[s, 1], 1, 1) + own_weight * v[s : s + 1]
        attended.append(jnp.sum(jnp.where(own_lane, mixed, 0.0), axis=0, keepdims=True))
    results[me] = jnp.concatenate(attended, axis=0).astype(BF16)
    exchange(results, send2, recv2)
    every = results[...].astype(F32).reshape(n * slots, local).astype(BF16)
    out_ref[...] = dot(back_ref[...], every, 1, 0).astype(BF16)


def decode(n, dec, pick, back, cosine, sine, bias, cache):
    _, slots, local = dec.shape
    return pl.pallas_call(
        functools.partial(decode_kernel, n),
        in_specs=[VSPEC] * 6 + [ASPEC],
        out_specs=VSPEC,
        out_shape=jax.ShapeDtypeStruct((slots, local), BF16),
        scratch_shapes=[
            VMEM((n, 3, slots, local), BF16),
            VMEM((n, slots, local), BF16),
            VMEM(cache.shape, BF16),
            pltpu.SemaphoreType.DMA(()),
        ]
        + [pltpu.SemaphoreType.DMA((n,))] * 4,
        compiler_params=pltpu.CompilerParams(
            collective_id=0, has_side_effects=True, vmem_limit_bytes=32 * MIB
        ),
        name="decode",
    )(dec, pick, back, cosine, sine, bias, cache)


def prefill_kernel(chunk, q_ref, nk_ref, nv_ref, ck_ref, cv_ref, bias_ref, out_ref):
    rows = q_ref.shape[2]
    for start in range(0, rows, chunk):
        stop = start + chunk
        q = q_ref[0, :, start:stop]
        cached = dot(q, ck_ref[0], 0, 0) + bias_ref[...]
        causal = lax.broadcasted_iota(jnp.int32, (chunk, stop), 1) <= start + lax.broadcasted_iota(
            jnp.int32, (chunk, stop), 0
        )
        fresh = jnp.where(causal, dot(q, nk_ref[0, :, :stop], 0, 0), NEGATIVE)
        peak = jnp.maximum(
            jnp.max(cached, axis=-1, keepdims=True), jnp.max(fresh, axis=-1, keepdims=True)
        )
        cached = jnp.exp(cached - peak)
        fresh = jnp.exp(fresh - peak)
        scale = 1.0 / (
            jnp.sum(cached, axis=-1, keepdims=True) + jnp.sum(fresh, axis=-1, keepdims=True)
        )
        mixed = dot((cached * scale).astype(BF16), cv_ref[0], 1, 1)
        mixed += dot((fresh * scale).astype(BF16), nv_ref[0, :, :stop], 1, 1)
        out_ref[:, start:stop] = mixed.T.astype(BF16)


def prefill(projected, cache, bias):
    _, local, rows = projected.shape
    keys = cache.shape[2]
    head = lambda part, length: pl.BlockSpec((1, HEAD, length), lambda h: (part, h, 0))
    return pl.pallas_call(
        functools.partial(prefill_kernel, 256),
        grid=(local // HEAD,),
        in_specs=[
            head(0, rows), head(1, rows), head(2, rows), head(0, keys), head(1, keys),
            pl.BlockSpec((1, keys), lambda h: (0, 0)),
        ],
        out_specs=pl.BlockSpec((HEAD, rows), lambda h: (h, 0)),
        out_shape=jax.ShapeDtypeStruct((local, rows), BF16),
        compiler_params=pltpu.CompilerParams(vmem_limit_bytes=40 * MIB),
        name="prefill",
    )(projected, projected, projected, cache, cache, bias)


def output_kernel(
    att_ref, datt_ref, w_ref, tok_ref, dtok_ref, gain_ref,
    hid_ref, dhid_ref, nor_ref, dnor_ref,
    att, give, have, got1, pair, got2, done, got3, dec,
    s1, r1, s2, r2, s3, r3, sd, rd,
):
    rows = tok_ref.shape[0]
    half = rows // 2
    pieces, chunk = pair.shape[0], pair.shape[1]
    me = lax.axis_index("tp")
    side = lax.rem(me, 2)
    core = me + 1 - 2 * side
    across = lax.rem(me + 2, 4)
    mine = pl.multiple_of(side * half, half)
    other = pl.multiple_of((1 - side) * half, half)

    barrier = pltpu.get_barrier_semaphore()
    for step in range(1, 4):
        pl.semaphore_signal(barrier, inc=1, device_id={"tp": lax.rem(me + step, 4)}, device_id_type=MESH)
    pl.semaphore_wait(barrier, 3)

    def send(src, dst, ssem, rsem, to):
        return pltpu.make_async_remote_copy(
            src_ref=src, dst_ref=dst, send_sem=ssem, recv_sem=rsem,
            device_id={"tp": to}, device_id_type=MESH,
        )

    first = [send(give.at[j], got1.at[j], s1.at[j], r1.at[j], core) for j in range(pieces)]
    second = [send(pair.at[j], got2.at[j], s2.at[j], r2.at[j], across) for j in range(pieces)]
    third = [send(done.at[j], got3.at[j], s3.at[j], r3.at[j], core) for j in range(pieces)]
    small = [
        send(dec.at[me], dec.at[me], sd.at[step], rd.at[step], lax.rem(me + step, 4))
        for step in range(1, 4)
    ]

    att[...] = att_ref[...].astype(F32).T.astype(BF16)
    block = 2 * chunk
    for j in range(pieces // 2):
        part = jnp.dot(att[pl.ds(other + j * block, block), :], w_ref[...], preferred_element_type=F32)
        give[2 * j] = part[:chunk].astype(BF16)
        first[2 * j].start()
        give[2 * j + 1] = part[chunk:].astype(BF16)
        first[2 * j + 1].start()
    for j in range(pieces // 2):
        part = jnp.dot(att[pl.ds(mine + j * block, block), :], w_ref[...], preferred_element_type=F32)
        have[2 * j] = part[:chunk].astype(BF16)
        have[2 * j + 1] = part[chunk:].astype(BF16)
        for i in (2 * j, 2 * j + 1):
            first[i].wait_recv()
            pair[i] = (have[i].astype(F32) + got1[i].astype(F32)).astype(BF16)
            second[i].start()
    dec[me] = jnp.dot(datt_ref[...], w_ref[...], preferred_element_type=F32).astype(BF16)
    for copy in small:
        copy.start()
    for j in range(pieces):
        span = pl.ds(mine + j * chunk, chunk)
        second[j].wait_recv()
        combined = pair[j].astype(F32) + got2[j].astype(F32)
        hidden = (tok_ref[span, :].astype(F32) + combined).astype(BF16)
        done[j] = hidden
        third[j].start()
        hid_ref[span, :] = hidden
        nor_ref[span, :] = rms_rows(hidden.astype(F32), gain_ref[...])
        if j > 0:
            take(third[j - 1], got3, hid_ref, nor_ref, gain_ref, other, j - 1, chunk)
    take(third[pieces - 1], got3, hid_ref, nor_ref, gain_ref, other, pieces - 1, chunk)
    for copy in small:
        copy.wait_recv()
    total = dec[0].astype(F32) + dec[1].astype(F32) + dec[2].astype(F32) + dec[3].astype(F32)
    hidden = (dtok_ref[...].astype(F32) + total).astype(BF16)
    dhid_ref[...] = hidden
    dnor_ref[...] = rms_rows(hidden.astype(F32), gain_ref[...])
    for copy in first + second + third + small:
        copy.wait_send()


def take(copy, got, hid_ref, nor_ref, gain_ref, other, j, chunk):
    copy.wait_recv()
    span = pl.ds(other + j * chunk, chunk)
    hidden = got[j]
    hid_ref[span, :] = hidden
    nor_ref[span, :] = rms_rows(hidden.astype(F32), gain_ref[...])


def output(att, datt, w, tokens, decode_tokens, gain):
    rows, width = tokens.shape
    local = w.shape[0]
    drows = decode_tokens.shape[0]
    pieces = 4
    chunk = rows // 2 // pieces
    buffer = VMEM((pieces, chunk, width), BF16)
    sem = pltpu.SemaphoreType.DMA((pieces,))
    return pl.pallas_call(
        output_kernel,
        in_specs=[VSPEC] * 6,
        out_specs=[VSPEC] * 4,
        out_shape=[
            jax.ShapeDtypeStruct((rows, width), BF16),
            jax.ShapeDtypeStruct((drows, width), BF16),
            jax.ShapeDtypeStruct((rows, width), BF16),
            jax.ShapeDtypeStruct((drows, width), BF16),
        ],
        scratch_shapes=[VMEM((rows, local), BF16)]
        + [buffer] * 7
        + [VMEM((4, drows, width), BF16)]
        + [sem] * 6
        + [pltpu.SemaphoreType.DMA((4,))] * 2,
        compiler_params=pltpu.CompilerParams(
            collective_id=1, has_side_effects=True, vmem_limit_bytes=48 * MIB
        ),
        name="output",
    )(att, datt, w, tokens, decode_tokens, gain)


def local_step(
    n,
    prefill_tokens,
    decode_tokens,
    attention_gain,
    qkv_weight,
    out_weight,
    feedforward_gain,
    prefill_cache,
    prefill_offsets,
    decode_cache,
    decode_lengths,
    request_slot,
):
    rows, width = prefill_tokens.shape
    drows = decode_tokens.shape[0]
    exponent = jnp.arange(HALF, dtype=F32) * (2.0 / HEAD)
    frequency = (ROPE_BASE ** (-exponent))[:, None]
    positions = prefill_offsets[0].astype(F32) + jnp.arange(rows, dtype=F32)
    angles = frequency * positions[None, :]
    dangles = frequency * decode_lengths.astype(F32)[None, :]
    rank = lax.axis_index("seq")
    slots = jnp.arange(n * drows, dtype=jnp.int32)
    own = rank * drows + jnp.arange(drows, dtype=jnp.int32)
    pick = (request_slot[None, :] == own[:, None]).astype(BF16)
    my_slots = lax.dynamic_slice_in_dim(request_slot, rank * drows, drows)
    back = (my_slots[:, None] == slots[None, :]).astype(BF16)
    dmax = decode_cache.shape[2]
    dbias = jnp.where(
        jnp.arange(dmax, dtype=jnp.int32)[None, :] < decode_lengths[:, None], 0.0, NEGATIVE
    ).astype(F32)[:, None, :]
    pmax = prefill_cache.shape[2]
    pbias = jnp.where(jnp.arange(pmax, dtype=jnp.int32) < prefill_offsets[0], 0.0, NEGATIVE).astype(F32)[None, :]

    projected, dec = project(
        prefill_tokens, decode_tokens, attention_gain[None, :], qkv_weight.transpose(1, 2, 0),
        jnp.cos(angles), jnp.sin(angles),
    )
    datt = decode(
        n, dec, pick, back, jnp.cos(dangles), jnp.sin(dangles), dbias,
        decode_cache.transpose(0, 1, 3, 2),
    )
    att = prefill(projected, prefill_cache[0].transpose(0, 2, 1), pbias)
    hidden, dhidden, normed, dnormed = output(
        att, datt, out_weight, prefill_tokens, decode_tokens, feedforward_gain[None, :]
    )
    return hidden, dhidden, normed, dnormed


def solution(mesh):
    placed = (
        P("seq", None),
        P("seq", None),
        P(),
        P(None, None, "tp"),
        P("tp", None),
        P(),
        P("seq", None, None, "tp"),
        P("seq"),
        P("seq", None, None, "tp"),
        P("seq"),
        P(),
    )
    return jax.shard_map(
        functools.partial(local_step, mesh.shape["seq"]),
        mesh=mesh,
        in_specs=placed,
        out_specs=(P("seq", None), P("seq", None), P("seq", None), P("seq", None)),
        check_vma=False,
    )
```

```python
import functools

import jax
import jax.numpy as jnp
from jax import lax
from jax.experimental import pallas as pl
from jax.experimental.pallas import tpu as pltpu
from jax.sharding import PartitionSpec as P

HEAD = 64
HALF = HEAD // 2
RMS_EPSILON = 1e-05
ROPE_BASE = 10000.0
NEGATIVE = -1e30
MIB = 1 << 20
F32, BF16 = jnp.float32, jnp.bfloat16
MESH = pl.DeviceIdType.MESH
VMEM = pltpu.VMEM
VSPEC = pl.BlockSpec(memory_space=pltpu.VMEM)
HSPEC = pl.BlockSpec(memory_space=pltpu.HBM)
SSPEC = pl.BlockSpec(memory_space=pltpu.SMEM)


def dot(a, b, ca, cb):
    return lax.dot_general(a, b, (((ca,), (cb,)), ((), ())), preferred_element_type=F32)


def rms_rows(x, gain):
    inverse = lax.rsqrt(jnp.mean(x * x, axis=-1, keepdims=True) + RMS_EPSILON)
    return (x * inverse * gain).astype(BF16)


def rotate_columns(x, cosine, sine, scale):
    pieces = []
    for head in range(x.shape[0] // HEAD):
        a = x[head * HEAD : head * HEAD + HALF]
        b = x[head * HEAD + HALF : (head + 1) * HEAD]
        pieces.append(a * cosine - b * sine)
        pieces.append(b * cosine + a * sine)
    turned = jnp.concatenate(pieces, axis=0).astype(BF16)
    return turned if scale is None else (turned.astype(F32) * scale).astype(BF16)


def project_kernel(
    gain_ref, cos_ref, sin_ref, tok_hbm, dtok_hbm, w_hbm, out_ref, dec_ref,
    tok, dtok, w, normed, dnormed, tok_sem, dtok_sem, w_sem,
):
    rows = tok.shape[0]
    loads = [pltpu.make_async_copy(w_hbm.at[part], w.at[part], w_sem.at[part]) for part in range(3)]
    tok_load = pltpu.make_async_copy(tok_hbm, tok, tok_sem)
    dtok_load = pltpu.make_async_copy(dtok_hbm, dtok, dtok_sem)
    tok_load.start()
    dtok_load.start()
    for load in loads:
        load.start()
    gain = gain_ref[...].reshape(1, gain_ref.shape[0])
    tok_load.wait()

    @pl.loop(0, rows // 64)
    def _(i):
        span = pl.ds(pl.multiple_of(i * 64, 64), 64)
        normed[span, :] = rms_rows(tok[span, :].astype(F32), gain)

    dtok_load.wait()
    dnormed[...] = rms_rows(dtok[...].astype(F32), gain)
    for part in range(3):
        loads[part].wait()
        product = dot(w[part], normed[...], 1, 1).astype(BF16)
        dec_ref[part] = dot(dnormed[...], w[part], 1, 1).astype(BF16)
        if part < 2:
            product = rotate_columns(
                product.astype(F32), cos_ref[:, :rows], sin_ref[:, :rows], 0.125 if part == 0 else None
            )
        out_ref[part] = product


def project(tokens, decode_tokens, gain, w, cosine, sine):
    rows, width = tokens.shape
    drows = decode_tokens.shape[0]
    local = w.shape[1]
    return pl.pallas_call(
        project_kernel,
        in_specs=[VSPEC] * 3 + [HSPEC] * 3,
        out_specs=[VSPEC] * 2,
        out_shape=[
            jax.ShapeDtypeStruct((3, local, rows), BF16),
            jax.ShapeDtypeStruct((3, drows, local), BF16),
        ],
        scratch_shapes=[
            VMEM((rows, width), BF16),
            VMEM((drows, width), BF16),
            VMEM((3, local, width), BF16),
            VMEM((rows, width), BF16),
            VMEM((drows, width), BF16),
            pltpu.SemaphoreType.DMA(()),
            pltpu.SemaphoreType.DMA(()),
            pltpu.SemaphoreType.DMA((3,)),
        ],
        compiler_params=pltpu.CompilerParams(vmem_limit_bytes=48 * MIB),
        name="project",
    )(gain, cosine, sine, tokens, decode_tokens, w)


def attention_kernel(
    n, proj_ref, dec_ref, cos_ref, sin_ref, slot_ref, offset_ref, length_ref,
    pcache_hbm, dcache_hbm, w_hbm, tok_hbm, dtok_hbm,
    hid_ref, dhid_ref,
    arrived, results, routed, pcache, dcache, w, tok, dtok, att, part, got1, pair, got2, dec,
    load_sem, send1, recv1, send2, recv2, s1, r1, s2, r2, s3, r3, sd, rd,
):
    slots, local = dec_ref.shape[1:]
    heads = local // HEAD
    rows = tok.shape[0]
    pieces, chunk = part.shape[:2]
    own_rows = chunk // 2
    keys = pcache.shape[2]
    dkeys = dcache.shape[3]
    seq = lax.axis_index("seq")
    tp = lax.axis_index("tp")
    side = lax.rem(tp, 2)
    core = tp + 1 - 2 * side
    across = lax.rem(tp + 2, 4)
    mine = pl.multiple_of(side * own_rows, own_rows)
    other = pl.multiple_of((1 - side) * own_rows, own_rows)

    loads = [
        pltpu.make_async_copy(src, dst, load_sem.at[i])
        for i, (src, dst) in enumerate(
            ((pcache_hbm, pcache), (w_hbm, w), (dcache_hbm, dcache), (tok_hbm, tok), (dtok_hbm, dtok))
        )
    ]
    for load in loads:
        load.start()

    barrier = pltpu.get_barrier_semaphore()
    for step in range(1, n):
        pl.semaphore_signal(barrier, inc=1, device_id={"seq": lax.rem(seq + step, n)}, device_id_type=MESH)
    for step in range(1, 4):
        pl.semaphore_signal(barrier, inc=1, device_id={"tp": lax.rem(tp + step, 4)}, device_id_type=MESH)
    pl.semaphore_wait(barrier, n + 2)

    def spread(buffer, send, recv):
        return [
            pltpu.make_async_remote_copy(
                src_ref=buffer.at[seq],
                dst_ref=buffer.at[seq],
                send_sem=send.at[step],
                recv_sem=recv.at[step],
                device_id={"seq": lax.rem(seq + step, n)},
                device_id_type=MESH,
            )
            for step in range(1, n)
        ]

    def send(src, dst, ssem, rsem, to):
        return pltpu.make_async_remote_copy(
            src_ref=src, dst_ref=dst, send_sem=ssem, recv_sem=rsem,
            device_id={"tp": to}, device_id_type=MESH,
        )

    def owned(c):
        return pl.ds(c * chunk + mine, own_rows)

    there = spread(arrived, send1, recv1)
    back = spread(results, send2, recv2)
    first = [
        send(part.at[c, pl.ds(other, own_rows)], got1.at[c], s1.at[c], r1.at[c], core) for c in range(pieces)
    ]
    second = [send(pair.at[c], got2.at[c], s2.at[c], r2.at[c], across) for c in range(pieces)]
    third = [send(hid_ref.at[owned(c)], hid_ref.at[owned(c)], s3.at[c], r3.at[c], core) for c in range(pieces)]
    small = [
        send(dec.at[tp], dec.at[tp], sd.at[step], rd.at[step], lax.rem(tp + step, 4)) for step in range(1, 4)
    ]

    arrived[seq] = dec_ref[...]
    for copy in there:
        copy.start()

    def cross(c):
        first[c].wait_recv()
        pair[c] = (part[c, pl.ds(mine, own_rows)].astype(F32) + got1[c].astype(F32)).astype(BF16)
        second[c].start()

    loads[0].wait()
    bias = jnp.where(lax.broadcasted_iota(jnp.int32, (1, keys), 1) < offset_ref[0], 0.0, NEGATIVE)
    for c in range(pieces):
        start, stop = c * chunk, (c + 1) * chunk

        @pl.loop(0, heads // 3)
        def _(group):
            for i in range(3):
                head = pl.ds(pl.multiple_of(group * (3 * HEAD) + i * HEAD, HEAD), HEAD)
                q = proj_ref[0, head, start:stop]
                cached = dot(q, pcache[0, head, :], 0, 0) + bias
                causal = lax.broadcasted_iota(jnp.int32, (chunk, stop), 1) <= start + lax.broadcasted_iota(
                    jnp.int32, (chunk, stop), 0
                )
                fresh = jnp.where(causal, dot(q, proj_ref[1, head, :stop], 0, 0), NEGATIVE)
                peak = jnp.maximum(
                    jnp.max(cached, axis=-1, keepdims=True), jnp.max(fresh, axis=-1, keepdims=True)
                )
                cached = jnp.exp(cached - peak)
                fresh = jnp.exp(fresh - peak)
                scale = 1.0 / (
                    jnp.sum(cached, axis=-1, keepdims=True) + jnp.sum(fresh, axis=-1, keepdims=True)
                )
                mixed = dot((cached * scale).astype(BF16), pcache[1, head, :], 1, 1)
                mixed += dot((fresh * scale).astype(BF16), proj_ref[2, head, :stop], 1, 1)
                att[head, :] = mixed.T.astype(BF16)
            if c > 0:

                @pl.when(group == 0)
                def _():
                    cross(c - 1)

        if c == 0:
            loads[1].wait()
        part[c] = dot(att[...], w[...], 0, 0).astype(BF16)
        first[c].start()

    for copy in there:
        copy.wait()
    cross(pieces - 1)
    loads[3].wait()

    def finish(c):
        second[c].wait_recv()
        combined = pair[c].astype(F32) + got2[c].astype(F32)
        hid_ref[owned(c), :] = (tok[owned(c), :].astype(F32) + combined).astype(BF16)
        third[c].start()

    total = n * slots
    chosen = seq * slots + lax.broadcasted_iota(jnp.int32, (slots, total), 0)
    slot_row = slot_ref[...].reshape(1, total)
    pick = (slot_row == chosen).astype(F32).astype(BF16)
    placing = (slot_row == lax.broadcasted_iota(jnp.int32, (total, total), 0)).astype(F32).astype(BF16)

    def gathered(which):
        return arrived[:, which].astype(F32).reshape(total, local).astype(BF16)

    dcos, dsin = cos_ref[:, rows:], sin_ref[:, rows:]
    q = rotate_columns(dot(gathered(0), pick, 0, 1).astype(BF16).astype(F32), dcos, dsin, 0.125).astype(F32)
    k = rotate_columns(dot(gathered(1), pick, 0, 1).astype(BF16).astype(F32), dcos, dsin, None).astype(F32)
    v = dot(pick, gathered(2), 1, 0).astype(BF16).astype(F32)
    padded = 16
    own_head = (
        lax.broadcasted_iota(jnp.int32, (local, padded), 0) // HEAD
        == lax.broadcasted_iota(jnp.int32, (local, padded), 1)
    )
    own_lane = (
        lax.broadcasted_iota(jnp.int32, (padded, local), 1) // HEAD
        == lax.broadcasted_iota(jnp.int32, (padded, local), 0)
    )
    loads[2].wait()
    position = lax.broadcasted_iota(jnp.int32, (1, dkeys), 1)
    attended = []
    for s in range(slots):
        query = jnp.where(own_head, q[:, s : s + 1], 0.0).astype(BF16)
        key = jnp.broadcast_to(k[:, s : s + 1], (local, 128)).astype(BF16)
        scores = dot(query, dcache[s, 0], 0, 0) + jnp.where(position < length_ref[s], 0.0, NEGATIVE)
        own = dot(query, key, 0, 0)[:, :1]
        peak = jnp.maximum(jnp.max(scores, axis=-1, keepdims=True), own)
        exps = jnp.exp(scores - peak)
        own_exp = jnp.exp(own - peak)
        denominator = jnp.sum(exps, axis=-1, keepdims=True) + own_exp
        weights = (exps / denominator).astype(BF16)
        own_weight = (own_exp / denominator).astype(BF16).astype(F32)
        mixed = dot(weights, dcache[s, 1], 1, 1) + own_weight * v[s : s + 1]
        attended.append(jnp.sum(jnp.where(own_lane, mixed, 0.0), axis=0, keepdims=True))
    results[seq] = jnp.concatenate(attended, axis=0).astype(BF16)
    for copy in back:
        copy.start()
    for c in range(pieces - 1):
        finish(c)
    for copy in back:
        copy.wait()
    every = results[...].astype(F32).reshape(total, local).astype(BF16)
    routed[...] = dot(placing, every, 0, 0)
    returned = routed[pl.ds(pl.multiple_of(seq * slots, slots), slots), :].astype(BF16)
    dec[tp] = dot(returned, w[...], 1, 0).astype(BF16)
    for copy in small:
        copy.start()
    finish(pieces - 1)
    for copy in small:
        copy.wait_recv()
    loads[4].wait()
    combined = dec[0].astype(F32) + dec[1].astype(F32) + dec[2].astype(F32) + dec[3].astype(F32)
    dhid_ref[...] = (dtok[...].astype(F32) + combined).astype(BF16)
    for copy in third:
        copy.wait_recv()
    for copy in first + second + third + small:
        copy.wait_send()


def attention(n, projected, dec, cosine, sine, slot, offset, lengths, pcache, dcache, w, tokens, decode_tokens):
    rows, width = tokens.shape
    _, slots, local = dec.shape
    pieces = 4
    chunk = rows // pieces
    buffer = VMEM((pieces, chunk // 2, width), BF16)
    sem = pltpu.SemaphoreType.DMA((pieces,))
    return pl.pallas_call(
        functools.partial(attention_kernel, n),
        in_specs=[VSPEC] * 5 + [SSPEC] * 2 + [HSPEC] * 5,
        out_specs=[VSPEC] * 2,
        out_shape=[jax.ShapeDtypeStruct((rows, width), BF16), jax.ShapeDtypeStruct((slots, width), BF16)],
        scratch_shapes=[
            VMEM((n, 3, slots, local), BF16),
            VMEM((n, slots, local), BF16),
            VMEM((n * slots, local), F32),
            VMEM(pcache.shape, BF16),
            VMEM(dcache.shape, BF16),
            VMEM(w.shape, BF16),
            VMEM((rows, width), BF16),
            VMEM((slots, width), BF16),
            VMEM((local, chunk), BF16),
            VMEM((pieces, chunk, width), BF16),
            buffer, buffer, buffer,
            VMEM((4, slots, width), BF16),
            pltpu.SemaphoreType.DMA((5,)),
        ]
        + [pltpu.SemaphoreType.DMA((n,))] * 4
        + [sem] * 6
        + [pltpu.SemaphoreType.DMA((4,))] * 2,
        compiler_params=pltpu.CompilerParams(
            collective_id=0, has_side_effects=True, vmem_limit_bytes=48 * MIB
        ),
        name="attention",
    )(projected, dec, cosine, sine, slot, offset, lengths, pcache, dcache, w, tokens, decode_tokens)


def norm_kernel(gain_ref, in_ref, din_ref, hid_ref, dhid_ref, nor_ref, dnor_ref):
    gain = gain_ref[...].reshape(1, gain_ref.shape[0])
    hidden = in_ref[...]
    hid_ref[...] = hidden
    nor_ref[...] = rms_rows(hidden.astype(F32), gain)

    @pl.when(pl.program_id(0) == 0)
    def _():
        dhidden = din_ref[...]
        dhid_ref[...] = dhidden
        dnor_ref[...] = rms_rows(dhidden.astype(F32), gain)


def final_norm(gain, hidden, dhidden):
    rows, width = hidden.shape
    block = 128
    tile = pl.BlockSpec((block, width), lambda i: (i, 0))
    small = pl.BlockSpec(dhidden.shape, lambda i: (0, 0))
    return pl.pallas_call(
        norm_kernel,
        grid=(rows // block,),
        in_specs=[pl.BlockSpec((width,), lambda i: (0,)), tile, small],
        out_specs=[tile, small, tile, small],
        out_shape=[jax.ShapeDtypeStruct(x.shape, BF16) for x in (hidden, dhidden, hidden, dhidden)],
        compiler_params=pltpu.CompilerParams(vmem_limit_bytes=32 * MIB),
        name="final_norm",
    )(gain, hidden, dhidden)


def local_step(
    n,
    prefill_tokens,
    decode_tokens,
    attention_gain,
    qkv_weight,
    out_weight,
    feedforward_gain,
    prefill_cache,
    prefill_offsets,
    decode_cache,
    decode_lengths,
    request_slot,
):
    rows = prefill_tokens.shape[0]
    exponent = jnp.arange(HALF, dtype=F32) * (2.0 / HEAD)
    frequency = (ROPE_BASE ** (-exponent))[:, None]
    positions = jnp.concatenate(
        [prefill_offsets[0].astype(F32) + jnp.arange(rows, dtype=F32), decode_lengths.astype(F32)]
    )
    angles = frequency * positions[None, :]
    cosine, sine = jnp.cos(angles), jnp.sin(angles)
    projected, dec = project(
        prefill_tokens, decode_tokens, attention_gain, qkv_weight.transpose(1, 2, 0), cosine, sine
    )
    hidden, dhidden = attention(
        n, projected, dec, cosine, sine, request_slot, prefill_offsets, decode_lengths,
        prefill_cache[0].transpose(0, 2, 1), decode_cache.transpose(0, 1, 3, 2), out_weight,
        prefill_tokens, decode_tokens,
    )
    hidden, dhidden, normed, dnormed = final_norm(feedforward_gain, hidden, dhidden)
    return hidden, dhidden, normed, dnormed


def solution(mesh):
    placed = (
        P("seq", None),
        P("seq", None),
        P(),
        P(None, None, "tp"),
        P("tp", None),
        P(),
        P("seq", None, None, "tp"),
        P("seq"),
        P("seq", None, None, "tp"),
        P("seq"),
        P(),
    )
    return jax.shard_map(
        functools.partial(local_step, mesh.shape["seq"]),
        mesh=mesh,
        in_specs=placed,
        out_specs=(P("seq", None), P("seq", None), P("seq", None), P("seq", None)),
        check_vma=False,
    )
```

```python
import functools

import jax
import jax.numpy as jnp
from jax import lax
from jax.experimental import pallas as pl
from jax.experimental.pallas import tpu as pltpu
from jax.sharding import PartitionSpec as P

HEAD = 64
HALF = HEAD // 2
RMS_EPSILON = 1e-05
ROPE_BASE = 10000.0
NEGATIVE = -1e30
MIB = 1 << 20
F32, BF16 = jnp.float32, jnp.bfloat16
MESH = pl.DeviceIdType.MESH
VMEM = pltpu.VMEM
VSPEC = pl.BlockSpec(memory_space=pltpu.VMEM)
HSPEC = pl.BlockSpec(memory_space=pltpu.HBM)
SSPEC = pl.BlockSpec(memory_space=pltpu.SMEM)


def dot(a, b, ca, cb):
    return lax.dot_general(a, b, (((ca,), (cb,)), ((), ())), preferred_element_type=F32)


def rms_rows(x, gain):
    inverse = lax.rsqrt(jnp.mean(x * x, axis=-1, keepdims=True) + RMS_EPSILON)
    return (x * inverse * gain).astype(BF16)


def rotate_columns(x, cosine, sine, scale):
    pieces = []
    for head in range(x.shape[0] // HEAD):
        a = x[head * HEAD : head * HEAD + HALF]
        b = x[head * HEAD + HALF : (head + 1) * HEAD]
        pieces.append(a * cosine - b * sine)
        pieces.append(b * cosine + a * sine)
    turned = jnp.concatenate(pieces, axis=0).astype(BF16)
    return turned if scale is None else (turned.astype(F32) * scale).astype(BF16)


def project_kernel(
    gain_ref, cos_ref, sin_ref, tok_hbm, dtok_hbm, w_hbm, out_ref, dec_ref,
    tok, dtok, w, normed, dnormed, tok_sem, dtok_sem, w_sem,
):
    rows = tok.shape[0]
    loads = [pltpu.make_async_copy(w_hbm.at[part], w.at[part], w_sem.at[part]) for part in range(3)]
    tok_load = pltpu.make_async_copy(tok_hbm, tok, tok_sem)
    dtok_load = pltpu.make_async_copy(dtok_hbm, dtok, dtok_sem)
    tok_load.start()
    dtok_load.start()
    for load in loads:
        load.start()
    gain = gain_ref[...].reshape(1, gain_ref.shape[0])
    tok_load.wait()

    @pl.loop(0, rows // 64)
    def _(i):
        span = pl.ds(pl.multiple_of(i * 64, 64), 64)
        normed[span, :] = rms_rows(tok[span, :].astype(F32), gain)

    dtok_load.wait()
    dnormed[...] = rms_rows(dtok[...].astype(F32), gain)
    for part in range(3):
        loads[part].wait()
        product = dot(w[part], normed[...], 1, 1).astype(BF16)
        dec_ref[part] = dot(dnormed[...], w[part], 1, 1).astype(BF16)
        if part < 2:
            product = rotate_columns(
                product.astype(F32), cos_ref[:, :rows], sin_ref[:, :rows], 0.125 if part == 0 else None
            )
        out_ref[part] = product


def project(tokens, decode_tokens, gain, w, cosine, sine):
    rows, width = tokens.shape
    drows = decode_tokens.shape[0]
    local = w.shape[1]
    return pl.pallas_call(
        project_kernel,
        in_specs=[VSPEC] * 3 + [HSPEC] * 3,
        out_specs=[VSPEC] * 2,
        out_shape=[
            jax.ShapeDtypeStruct((3, local, rows), BF16),
            jax.ShapeDtypeStruct((3, drows, local), BF16),
        ],
        scratch_shapes=[
            VMEM((rows, width), BF16),
            VMEM((drows, width), BF16),
            VMEM((3, local, width), BF16),
            VMEM((rows, width), BF16),
            VMEM((drows, width), BF16),
            pltpu.SemaphoreType.DMA(()),
            pltpu.SemaphoreType.DMA(()),
            pltpu.SemaphoreType.DMA((3,)),
        ],
        compiler_params=pltpu.CompilerParams(vmem_limit_bytes=59 * MIB),
        name="project",
    )(gain, cosine, sine, tokens, decode_tokens, w)


def attention_kernel(
    n, proj_hbm, dec_hbm, cos_ref, sin_ref, slot_ref, offset_ref, length_ref,
    pcache_hbm, dcache_hbm, w_hbm, tok_hbm, dtok_hbm,
    hid_ref, dhid_ref,
    arrived, results, routed, proj_ref, pcache, dcache, w, tok, dtok, att, part, got1, pair, got2, dec,
    load_sem, send1, recv1, send2, recv2, s1, r1, s2, r2, s3, r3, sd, rd,
):
    slots, local = arrived.shape[2:]
    heads = local // HEAD
    rows = tok.shape[0]
    pieces, chunk = part.shape[:2]
    own_rows = chunk // 2
    keys = pcache.shape[2]
    dkeys = dcache.shape[3]
    seq = lax.axis_index("seq")
    tp = lax.axis_index("tp")
    side = lax.rem(tp, 2)
    core = tp + 1 - 2 * side
    across = lax.rem(tp + 2, 4)
    mine = pl.multiple_of(side * own_rows, own_rows)
    other = pl.multiple_of((1 - side) * own_rows, own_rows)

    loads = [
        pltpu.make_async_copy(src, dst, load_sem.at[i])
        for i, (src, dst) in enumerate(
            ((pcache_hbm, pcache), (w_hbm, w), (dcache_hbm, dcache), (tok_hbm, tok), (dtok_hbm, dtok))
        )
    ]
    dec_load = pltpu.make_async_copy(dec_hbm, arrived.at[seq], load_sem.at[5])
    proj_load = pltpu.make_async_copy(proj_hbm, proj_ref, load_sem.at[6])
    dec_load.start()
    proj_load.start()
    for load in loads:
        load.start()

    barrier = pltpu.get_barrier_semaphore()
    for step in range(1, n):
        pl.semaphore_signal(barrier, inc=1, device_id={"seq": lax.rem(seq + step, n)}, device_id_type=MESH)
    for step in range(1, 4):
        pl.semaphore_signal(barrier, inc=1, device_id={"tp": lax.rem(tp + step, 4)}, device_id_type=MESH)
    pl.semaphore_wait(barrier, n + 2)

    def spread(buffer, send, recv):
        return [
            pltpu.make_async_remote_copy(
                src_ref=buffer.at[seq],
                dst_ref=buffer.at[seq],
                send_sem=send.at[step],
                recv_sem=recv.at[step],
                device_id={"seq": lax.rem(seq + step, n)},
                device_id_type=MESH,
            )
            for step in range(1, n)
        ]

    def send(src, dst, ssem, rsem, to):
        return pltpu.make_async_remote_copy(
            src_ref=src, dst_ref=dst, send_sem=ssem, recv_sem=rsem,
            device_id={"tp": to}, device_id_type=MESH,
        )

    def owned(c):
        return pl.ds(c * chunk + mine, own_rows)

    there = spread(arrived, send1, recv1)
    back = spread(results, send2, recv2)
    first = [
        send(part.at[c, pl.ds(other, own_rows)], got1.at[c], s1.at[c], r1.at[c], core) for c in range(pieces)
    ]
    second = [send(pair.at[c], got2.at[c], s2.at[c], r2.at[c], across) for c in range(pieces)]
    third = [send(hid_ref.at[owned(c)], hid_ref.at[owned(c)], s3.at[c], r3.at[c], core) for c in range(pieces)]
    small = [
        send(dec.at[tp], dec.at[tp], sd.at[step], rd.at[step], lax.rem(tp + step, 4)) for step in range(1, 4)
    ]

    dec_load.wait()
    for copy in there:
        copy.start()

    def cross(c):
        first[c].wait_recv()
        pair[c] = (part[c, pl.ds(mine, own_rows)].astype(F32) + got1[c].astype(F32)).astype(BF16)
        second[c].start()

    proj_load.wait()
    loads[0].wait()
    bias = jnp.where(lax.broadcasted_iota(jnp.int32, (1, keys), 1) < offset_ref[0], 0.0, NEGATIVE)
    for c in range(pieces):
        start, stop = c * chunk, (c + 1) * chunk

        @pl.loop(0, heads // 3)
        def _(group):
            for i in range(3):
                head = pl.ds(pl.multiple_of(group * (3 * HEAD) + i * HEAD, HEAD), HEAD)
                q = proj_ref[0, head, start:stop]
                cached = dot(q, pcache[0, head, :], 0, 0) + bias
                causal = lax.broadcasted_iota(jnp.int32, (chunk, stop), 1) <= start + lax.broadcasted_iota(
                    jnp.int32, (chunk, stop), 0
                )
                fresh = jnp.where(causal, dot(q, proj_ref[1, head, :stop], 0, 0), NEGATIVE)
                peak = jnp.maximum(
                    jnp.max(cached, axis=-1, keepdims=True), jnp.max(fresh, axis=-1, keepdims=True)
                )
                cached = jnp.exp(cached - peak)
                fresh = jnp.exp(fresh - peak)
                scale = 1.0 / (
                    jnp.sum(cached, axis=-1, keepdims=True) + jnp.sum(fresh, axis=-1, keepdims=True)
                )
                mixed = dot((cached * scale).astype(BF16), pcache[1, head, :], 1, 1)
                mixed += dot((fresh * scale).astype(BF16), proj_ref[2, head, :stop], 1, 1)
                att[head, :] = mixed.T.astype(BF16)
            if c > 0:

                @pl.when(group == 0)
                def _():
                    cross(c - 1)

        if c == 0:
            loads[1].wait()
        part[c] = dot(att[...], w[...], 0, 0).astype(BF16)
        first[c].start()

    for copy in there:
        copy.wait()
    cross(pieces - 1)
    loads[3].wait()

    def finish(c):
        second[c].wait_recv()
        combined = pair[c].astype(F32) + got2[c].astype(F32)
        hid_ref[owned(c), :] = (tok[owned(c), :].astype(F32) + combined).astype(BF16)
        third[c].start()

    total = n * slots
    chosen = seq * slots + lax.broadcasted_iota(jnp.int32, (slots, total), 0)
    slot_row = slot_ref[...].reshape(1, total)
    pick = (slot_row == chosen).astype(F32).astype(BF16)
    placing = (slot_row == lax.broadcasted_iota(jnp.int32, (total, total), 0)).astype(F32).astype(BF16)

    def gathered(which):
        return arrived[:, which].astype(F32).reshape(total, local).astype(BF16)

    dcos, dsin = cos_ref[:, rows:], sin_ref[:, rows:]
    q = rotate_columns(dot(gathered(0), pick, 0, 1).astype(BF16).astype(F32), dcos, dsin, 0.125).astype(F32)
    k = rotate_columns(dot(gathered(1), pick, 0, 1).astype(BF16).astype(F32), dcos, dsin, None).astype(F32)
    v = dot(pick, gathered(2), 1, 0).astype(BF16).astype(F32)
    padded = 16
    own_head = (
        lax.broadcasted_iota(jnp.int32, (local, padded), 0) // HEAD
        == lax.broadcasted_iota(jnp.int32, (local, padded), 1)
    )
    own_lane = (
        lax.broadcasted_iota(jnp.int32, (padded, local), 1) // HEAD
        == lax.broadcasted_iota(jnp.int32, (padded, local), 0)
    )
    loads[2].wait()
    position = lax.broadcasted_iota(jnp.int32, (1, dkeys), 1)
    product = q * k
    own = jnp.concatenate(
        [
            jnp.sum(product[head * HEAD : (head + 1) * HEAD], axis=0, keepdims=True)
            if head < heads
            else jnp.zeros((1, slots), F32)
            for head in range(padded)
        ],
        axis=0,
    )
    own = jnp.concatenate([own[:, s : s + 1] for s in range(slots)], axis=0)
    scores = []
    for s in range(slots):
        query = jnp.where(own_head, q[:, s : s + 1], 0.0).astype(BF16)
        hidden_keys = jnp.where(position < length_ref[s], 0.0, NEGATIVE)
        scores.append(dot(query, dcache[s, 0], 0, 0) + hidden_keys)
    scores = jnp.concatenate(scores, axis=0)
    peak = jnp.maximum(jnp.max(scores, axis=-1, keepdims=True), own)
    exps = jnp.exp(scores - peak)
    own_exp = jnp.exp(own - peak)
    denominator = jnp.sum(exps, axis=-1, keepdims=True) + own_exp
    weights = (exps / denominator).astype(BF16)
    own_weight = (own_exp / denominator).astype(BF16).astype(F32)
    attended = []
    for s in range(slots):
        span = slice(s * padded, (s + 1) * padded)
        mixed = dot(weights[span], dcache[s, 1], 1, 1) + own_weight[span] * v[s : s + 1]
        attended.append(jnp.sum(jnp.where(own_lane, mixed, 0.0), axis=0, keepdims=True))
    results[seq] = jnp.concatenate(attended, axis=0).astype(BF16)
    for copy in back:
        copy.start()
    for c in range(pieces - 1):
        finish(c)
    for copy in back:
        copy.wait()
    every = results[...].astype(F32).reshape(total, local).astype(BF16)
    routed[...] = dot(placing, every, 0, 0)
    returned = routed[pl.ds(pl.multiple_of(seq * slots, slots), slots), :].astype(BF16)
    dec[tp] = dot(returned, w[...], 1, 0).astype(BF16)
    for copy in small:
        copy.start()
    finish(pieces - 1)
    for copy in small:
        copy.wait_recv()
    loads[4].wait()
    combined = dec[0].astype(F32) + dec[1].astype(F32) + dec[2].astype(F32) + dec[3].astype(F32)
    dhid_ref[...] = (dtok[...].astype(F32) + combined).astype(BF16)
    for copy in third:
        copy.wait_recv()
    for copy in first + second + third + small:
        copy.wait_send()


def attention(n, projected, dec, cosine, sine, slot, offset, lengths, pcache, dcache, w, tokens, decode_tokens):
    rows, width = tokens.shape
    _, slots, local = dec.shape
    pieces = 4
    chunk = rows // pieces
    buffer = VMEM((pieces, chunk // 2, width), BF16)
    sem = pltpu.SemaphoreType.DMA((pieces,))
    return pl.pallas_call(
        functools.partial(attention_kernel, n),
        in_specs=[HSPEC] * 2 + [VSPEC] * 3 + [SSPEC] * 2 + [HSPEC] * 5,
        out_specs=[VSPEC] * 2,
        out_shape=[jax.ShapeDtypeStruct((rows, width), BF16), jax.ShapeDtypeStruct((slots, width), BF16)],
        scratch_shapes=[
            VMEM((n, 3, slots, local), BF16),
            VMEM((n, slots, local), BF16),
            VMEM((n * slots, local), F32),
            VMEM(projected.shape, BF16),
            VMEM(pcache.shape, BF16),
            VMEM(dcache.shape, BF16),
            VMEM(w.shape, BF16),
            VMEM((rows, width), BF16),
            VMEM((slots, width), BF16),
            VMEM((local, chunk), BF16),
            VMEM((pieces, chunk, width), BF16),
            buffer, buffer, buffer,
            VMEM((4, slots, width), BF16),
            pltpu.SemaphoreType.DMA((7,)),
        ]
        + [pltpu.SemaphoreType.DMA((n,))] * 4
        + [sem] * 6
        + [pltpu.SemaphoreType.DMA((4,))] * 2,
        compiler_params=pltpu.CompilerParams(
            collective_id=0, has_side_effects=True, vmem_limit_bytes=48 * MIB
        ),
        name="attention",
    )(projected, dec, cosine, sine, slot, offset, lengths, pcache, dcache, w, tokens, decode_tokens)


def norm_kernel(gain_ref, in_ref, din_ref, hid_ref, dhid_ref, nor_ref, dnor_ref):
    gain = gain_ref[...].reshape(1, gain_ref.shape[0])
    hidden = in_ref[...]
    hid_ref[...] = hidden
    nor_ref[...] = rms_rows(hidden.astype(F32), gain)

    @pl.when(pl.program_id(0) == 0)
    def _():
        dhidden = din_ref[...]
        dhid_ref[...] = dhidden
        dnor_ref[...] = rms_rows(dhidden.astype(F32), gain)


def final_norm(gain, hidden, dhidden):
    rows, width = hidden.shape
    block = 128
    tile = pl.BlockSpec((block, width), lambda i: (i, 0))
    small = pl.BlockSpec(dhidden.shape, lambda i: (0, 0))
    return pl.pallas_call(
        norm_kernel,
        grid=(rows // block,),
        in_specs=[pl.BlockSpec((width,), lambda i: (0,)), tile, small],
        out_specs=[tile, small, tile, small],
        out_shape=[jax.ShapeDtypeStruct(x.shape, BF16) for x in (hidden, dhidden, hidden, dhidden)],
        compiler_params=pltpu.CompilerParams(vmem_limit_bytes=32 * MIB),
        name="final_norm",
    )(gain, hidden, dhidden)


def local_step(
    n,
    prefill_tokens,
    decode_tokens,
    attention_gain,
    qkv_weight,
    out_weight,
    feedforward_gain,
    prefill_cache,
    prefill_offsets,
    decode_cache,
    decode_lengths,
    request_slot,
):
    rows = prefill_tokens.shape[0]
    exponent = jnp.arange(HALF, dtype=F32) * (2.0 / HEAD)
    frequency = (ROPE_BASE ** (-exponent))[:, None]
    positions = jnp.concatenate(
        [prefill_offsets[0].astype(F32) + jnp.arange(rows, dtype=F32), decode_lengths.astype(F32)]
    )
    angles = frequency * positions[None, :]
    cosine, sine = jnp.cos(angles), jnp.sin(angles)
    projected, dec = project(
        prefill_tokens, decode_tokens, attention_gain, qkv_weight.transpose(1, 2, 0), cosine, sine
    )
    hidden, dhidden = attention(
        n, projected, dec, cosine, sine, request_slot, prefill_offsets, decode_lengths,
        prefill_cache[0].transpose(0, 2, 1), decode_cache.transpose(0, 1, 3, 2), out_weight,
        prefill_tokens, decode_tokens,
    )
    hidden, dhidden, normed, dnormed = final_norm(feedforward_gain, hidden, dhidden)
    return hidden, dhidden, normed, dnormed


def solution(mesh):
    placed = (
        P("seq", None),
        P("seq", None),
        P(),
        P(None, None, "tp"),
        P("tp", None),
        P(),
        P("seq", None, None, "tp"),
        P("seq"),
        P("seq", None, None, "tp"),
        P("seq"),
        P(),
    )
    return jax.shard_map(
        functools.partial(local_step, mesh.shape["seq"]),
        mesh=mesh,
        in_specs=placed,
        out_specs=(P("seq", None), P("seq", None), P("seq", None), P("seq", None)),
        check_vma=False,
    )
```

```python
import functools

import jax
import jax.numpy as jnp
from jax import lax
from jax.experimental import pallas as pl
from jax.experimental.pallas import tpu as pltpu
from jax.sharding import PartitionSpec as P

HEAD = 64
HALF = HEAD // 2
RMS_EPSILON = 1e-05
ROPE_BASE = 10000.0
NEGATIVE = -1e30
MIB = 1 << 20
F32, BF16 = jnp.float32, jnp.bfloat16
MESH = pl.DeviceIdType.MESH
VMEM = pltpu.VMEM
VSPEC = pl.BlockSpec(memory_space=pltpu.VMEM)
HSPEC = pl.BlockSpec(memory_space=pltpu.HBM)
SSPEC = pl.BlockSpec(memory_space=pltpu.SMEM)


def dot(a, b, ca, cb):
    return lax.dot_general(a, b, (((ca,), (cb,)), ((), ())), preferred_element_type=F32)


def rms_rows(x, gain):
    inverse = lax.rsqrt(jnp.mean(x * x, axis=-1, keepdims=True) + RMS_EPSILON)
    return (x * inverse * gain).astype(BF16)


def rotate_columns(x, cosine, sine, scale):
    pieces = []
    for head in range(x.shape[0] // HEAD):
        a = x[head * HEAD : head * HEAD + HALF]
        b = x[head * HEAD + HALF : (head + 1) * HEAD]
        pieces.append(a * cosine - b * sine)
        pieces.append(b * cosine + a * sine)
    turned = jnp.concatenate(pieces, axis=0).astype(BF16)
    return turned if scale is None else (turned.astype(F32) * scale).astype(BF16)


def project_kernel(
    gain_ref, cos_ref, sin_ref, tok, dtok, w_hbm, out_ref, dec_ref, w, normed, dnormed, w_sem,
):
    rows = tok.shape[0]
    loads = [pltpu.make_async_copy(w_hbm.at[part], w.at[part], w_sem.at[part]) for part in range(3)]
    for load in loads:
        load.start()
    gain = gain_ref[...].reshape(1, gain_ref.shape[0])

    @pl.loop(0, rows // 64)
    def _(i):
        span = pl.ds(pl.multiple_of(i * 64, 64), 64)
        normed[span, :] = rms_rows(tok[span, :].astype(F32), gain)

    dnormed[...] = rms_rows(dtok[...].astype(F32), gain)
    for part in range(3):
        loads[part].wait()
        product = dot(w[part], normed[...], 1, 1).astype(BF16)
        dec_ref[part] = dot(dnormed[...], w[part], 1, 1).astype(BF16)
        if part < 2:
            product = rotate_columns(
                product.astype(F32), cos_ref[:, :rows], sin_ref[:, :rows], 0.125 if part == 0 else None
            )
        out_ref[part] = product


def project(tokens, decode_tokens, gain, w, cosine, sine):
    rows, width = tokens.shape
    drows = decode_tokens.shape[0]
    local = w.shape[1]
    return pl.pallas_call(
        project_kernel,
        in_specs=[VSPEC] * 5 + [HSPEC],
        out_specs=[VSPEC] * 2,
        out_shape=[
            jax.ShapeDtypeStruct((3, local, rows), BF16),
            jax.ShapeDtypeStruct((3, drows, local), BF16),
        ],
        scratch_shapes=[
            VMEM((3, local, width), BF16),
            VMEM((rows, width), BF16),
            VMEM((drows, width), BF16),
            pltpu.SemaphoreType.DMA((3,)),
        ],
        compiler_params=pltpu.CompilerParams(vmem_limit_bytes=48 * MIB),
        name="project",
    )(gain, cosine, sine, tokens, decode_tokens, w)


def attention_kernel(
    n, proj_ref, dec_ref, cos_ref, sin_ref, slot_ref, offset_ref, length_ref,
    pcache_hbm, dcache_hbm, w_hbm, tok_hbm, dtok_hbm,
    hid_ref, dhid_ref,
    arrived, results, routed, pcache, dcache, w, tok, dtok, att, part, got1, pair, got2, dec,
    load_sem, send1, recv1, send2, recv2, s1, r1, s2, r2, s3, r3, sd, rd,
):
    slots, local = dec_ref.shape[1:]
    heads = local // HEAD
    rows = tok.shape[0]
    pieces, chunk = part.shape[:2]
    own_rows = chunk // 2
    keys = pcache.shape[2]
    dkeys = dcache.shape[3]
    seq = lax.axis_index("seq")
    tp = lax.axis_index("tp")
    side = lax.rem(tp, 2)
    core = tp + 1 - 2 * side
    across = lax.rem(tp + 2, 4)
    mine = pl.multiple_of(side * own_rows, own_rows)
    other = pl.multiple_of((1 - side) * own_rows, own_rows)

    loads = [
        pltpu.make_async_copy(src, dst, load_sem.at[i])
        for i, (src, dst) in enumerate(
            ((pcache_hbm, pcache), (w_hbm, w), (dcache_hbm, dcache), (tok_hbm, tok), (dtok_hbm, dtok))
        )
    ]
    for load in loads:
        load.start()

    barrier = pltpu.get_barrier_semaphore()
    for step in range(1, n):
        pl.semaphore_signal(barrier, inc=1, device_id={"seq": lax.rem(seq + step, n)}, device_id_type=MESH)
    for step in range(1, 4):
        pl.semaphore_signal(barrier, inc=1, device_id={"tp": lax.rem(tp + step, 4)}, device_id_type=MESH)
    pl.semaphore_wait(barrier, n + 2)

    def spread(buffer, send, recv):
        return [
            pltpu.make_async_remote_copy(
                src_ref=buffer.at[seq],
                dst_ref=buffer.at[seq],
                send_sem=send.at[step],
                recv_sem=recv.at[step],
                device_id={"seq": lax.rem(seq + step, n)},
                device_id_type=MESH,
            )
            for step in range(1, n)
        ]

    def send(src, dst, ssem, rsem, to):
        return pltpu.make_async_remote_copy(
            src_ref=src, dst_ref=dst, send_sem=ssem, recv_sem=rsem,
            device_id={"tp": to}, device_id_type=MESH,
        )

    def owned(c):
        return pl.ds(c * chunk + mine, own_rows)

    there = spread(arrived, send1, recv1)
    back = spread(results, send2, recv2)
    first = [
        send(part.at[c, pl.ds(other, own_rows)], got1.at[c], s1.at[c], r1.at[c], core) for c in range(pieces)
    ]
    second = [send(pair.at[c], got2.at[c], s2.at[c], r2.at[c], across) for c in range(pieces)]
    third = [send(hid_ref.at[owned(c)], hid_ref.at[owned(c)], s3.at[c], r3.at[c], core) for c in range(pieces)]
    small = [
        send(dec.at[tp], dec.at[tp], sd.at[step], rd.at[step], lax.rem(tp + step, 4)) for step in range(1, 4)
    ]

    arrived[seq] = dec_ref[...]
    for copy in there:
        copy.start()

    def cross(c):
        first[c].wait_recv()
        pair[c] = (part[c, pl.ds(mine, own_rows)].astype(F32) + got1[c].astype(F32)).astype(BF16)
        second[c].start()

    loads[0].wait()
    bias = jnp.where(lax.broadcasted_iota(jnp.int32, (1, keys), 1) < offset_ref[0], 0.0, NEGATIVE)
    for c in range(pieces):
        start, stop = c * chunk, (c + 1) * chunk

        @pl.loop(0, heads // 3)
        def _(group):
            for i in range(3):
                head = pl.ds(pl.multiple_of(group * (3 * HEAD) + i * HEAD, HEAD), HEAD)
                q = proj_ref[0, head, start:stop]
                cached = dot(q, pcache[0, head, :], 0, 0) + bias
                causal = lax.broadcasted_iota(jnp.int32, (chunk, stop), 1) <= start + lax.broadcasted_iota(
                    jnp.int32, (chunk, stop), 0
                )
                fresh = jnp.where(causal, dot(q, proj_ref[1, head, :stop], 0, 0), NEGATIVE)
                peak = jnp.maximum(
                    jnp.max(cached, axis=-1, keepdims=True), jnp.max(fresh, axis=-1, keepdims=True)
                )
                cached = jnp.exp(cached - peak)
                fresh = jnp.exp(fresh - peak)
                scale = 1.0 / (
                    jnp.sum(cached, axis=-1, keepdims=True) + jnp.sum(fresh, axis=-1, keepdims=True)
                )
                mixed = dot((cached * scale).astype(BF16), pcache[1, head, :], 1, 1)
                mixed += dot((fresh * scale).astype(BF16), proj_ref[2, head, :stop], 1, 1)
                att[head, :] = mixed.T.astype(BF16)
            if c > 0:

                @pl.when(group == 0)
                def _():
                    cross(c - 1)

        if c == 0:
            loads[1].wait()
        part[c] = dot(att[...], w[...], 0, 0).astype(BF16)
        first[c].start()

    for copy in there:
        copy.wait()
    cross(pieces - 1)
    loads[3].wait()

    def finish(c):
        second[c].wait_recv()
        combined = pair[c].astype(F32) + got2[c].astype(F32)
        hid_ref[owned(c), :] = (tok[owned(c), :].astype(F32) + combined).astype(BF16)
        third[c].start()

    total = n * slots
    chosen = seq * slots + lax.broadcasted_iota(jnp.int32, (slots, total), 0)
    slot_row = slot_ref[...].reshape(1, total)
    pick = (slot_row == chosen).astype(F32).astype(BF16)
    placing = (slot_row == lax.broadcasted_iota(jnp.int32, (total, total), 0)).astype(F32).astype(BF16)

    def gathered(which):
        return arrived[:, which].astype(F32).reshape(total, local).astype(BF16)

    dcos, dsin = cos_ref[:, rows:], sin_ref[:, rows:]
    q = rotate_columns(dot(gathered(0), pick, 0, 1).astype(BF16).astype(F32), dcos, dsin, 0.125).astype(F32)
    k = rotate_columns(dot(gathered(1), pick, 0, 1).astype(BF16).astype(F32), dcos, dsin, None).astype(F32)
    v = dot(pick, gathered(2), 1, 0).astype(BF16).astype(F32)
    padded = 16
    own_head = (
        lax.broadcasted_iota(jnp.int32, (local, padded), 0) // HEAD
        == lax.broadcasted_iota(jnp.int32, (local, padded), 1)
    )
    own_lane = (
        lax.broadcasted_iota(jnp.int32, (padded, local), 1) // HEAD
        == lax.broadcasted_iota(jnp.int32, (padded, local), 0)
    )
    loads[2].wait()
    position = lax.broadcasted_iota(jnp.int32, (1, dkeys), 1)
    product = q * k
    own = jnp.concatenate(
        [
            jnp.sum(product[head * HEAD : (head + 1) * HEAD], axis=0, keepdims=True)
            if head < heads
            else jnp.zeros((1, slots), F32)
            for head in range(padded)
        ],
        axis=0,
    )
    own = jnp.concatenate([own[:, s : s + 1] for s in range(slots)], axis=0)
    scores = []
    for s in range(slots):
        query = jnp.where(own_head, q[:, s : s + 1], 0.0).astype(BF16)
        hidden_keys = jnp.where(position < length_ref[s], 0.0, NEGATIVE)
        scores.append(dot(query, dcache[s, 0], 0, 0) + hidden_keys)
    scores = jnp.concatenate(scores, axis=0)
    peak = jnp.maximum(jnp.max(scores, axis=-1, keepdims=True), own)
    exps = jnp.exp(scores - peak)
    own_exp = jnp.exp(own - peak)
    denominator = jnp.sum(exps, axis=-1, keepdims=True) + own_exp
    weights = (exps / denominator).astype(BF16)
    own_weight = (own_exp / denominator).astype(BF16).astype(F32)
    attended = []
    for s in range(slots):
        span = slice(s * padded, (s + 1) * padded)
        mixed = dot(weights[span], dcache[s, 1], 1, 1) + own_weight[span] * v[s : s + 1]
        attended.append(jnp.sum(jnp.where(own_lane, mixed, 0.0), axis=0, keepdims=True))
    results[seq] = jnp.concatenate(attended, axis=0).astype(BF16)
    for copy in back:
        copy.start()
    for c in range(pieces - 1):
        finish(c)
    for copy in back:
        copy.wait()
    every = results[...].astype(F32).reshape(total, local).astype(BF16)
    routed[...] = dot(placing, every, 0, 0)
    returned = routed[pl.ds(pl.multiple_of(seq * slots, slots), slots), :].astype(BF16)
    dec[tp] = dot(returned, w[...], 1, 0).astype(BF16)
    for copy in small:
        copy.start()
    finish(pieces - 1)
    for copy in small:
        copy.wait_recv()
    loads[4].wait()
    combined = dec[0].astype(F32) + dec[1].astype(F32) + dec[2].astype(F32) + dec[3].astype(F32)
    dhid_ref[...] = (dtok[...].astype(F32) + combined).astype(BF16)
    for copy in third:
        copy.wait_recv()
    for copy in first + second + third + small:
        copy.wait_send()


def attention(n, projected, dec, cosine, sine, slot, offset, lengths, pcache, dcache, w, tokens, decode_tokens):
    rows, width = tokens.shape
    _, slots, local = dec.shape
    pieces = 4
    chunk = rows // pieces
    buffer = VMEM((pieces, chunk // 2, width), BF16)
    sem = pltpu.SemaphoreType.DMA((pieces,))
    return pl.pallas_call(
        functools.partial(attention_kernel, n),
        in_specs=[VSPEC] * 5 + [SSPEC] * 2 + [HSPEC] * 5,
        out_specs=[VSPEC] * 2,
        out_shape=[jax.ShapeDtypeStruct((rows, width), BF16), jax.ShapeDtypeStruct((slots, width), BF16)],
        scratch_shapes=[
            VMEM((n, 3, slots, local), BF16),
            VMEM((n, slots, local), BF16),
            VMEM((n * slots, local), F32),
            VMEM(pcache.shape, BF16),
            VMEM(dcache.shape, BF16),
            VMEM(w.shape, BF16),
            VMEM((rows, width), BF16),
            VMEM((slots, width), BF16),
            VMEM((local, chunk), BF16),
            VMEM((pieces, chunk, width), BF16),
            buffer, buffer, buffer,
            VMEM((4, slots, width), BF16),
            pltpu.SemaphoreType.DMA((5,)),
        ]
        + [pltpu.SemaphoreType.DMA((n,))] * 4
        + [sem] * 6
        + [pltpu.SemaphoreType.DMA((4,))] * 2,
        compiler_params=pltpu.CompilerParams(
            collective_id=0, has_side_effects=True, vmem_limit_bytes=48 * MIB
        ),
        name="attention",
    )(projected, dec, cosine, sine, slot, offset, lengths, pcache, dcache, w, tokens, decode_tokens)


def norm_kernel(gain_ref, in_ref, din_ref, hid_ref, dhid_ref, nor_ref, dnor_ref):
    gain = gain_ref[...].reshape(1, gain_ref.shape[0])
    hidden = in_ref[...]
    hid_ref[...] = hidden
    nor_ref[...] = rms_rows(hidden.astype(F32), gain)

    @pl.when(pl.program_id(0) == 0)
    def _():
        dhidden = din_ref[...]
        dhid_ref[...] = dhidden
        dnor_ref[...] = rms_rows(dhidden.astype(F32), gain)


def final_norm(gain, hidden, dhidden):
    rows, width = hidden.shape
    block = 128
    tile = pl.BlockSpec((block, width), lambda i: (i, 0))
    small = pl.BlockSpec(dhidden.shape, lambda i: (0, 0))
    return pl.pallas_call(
        norm_kernel,
        grid=(rows // block,),
        in_specs=[pl.BlockSpec((width,), lambda i: (0,)), tile, small],
        out_specs=[tile, small, tile, small],
        out_shape=[jax.ShapeDtypeStruct(x.shape, BF16) for x in (hidden, dhidden, hidden, dhidden)],
        compiler_params=pltpu.CompilerParams(vmem_limit_bytes=32 * MIB),
        name="final_norm",
    )(gain, hidden, dhidden)


def local_step(
    n,
    prefill_tokens,
    decode_tokens,
    attention_gain,
    qkv_weight,
    out_weight,
    feedforward_gain,
    prefill_cache,
    prefill_offsets,
    decode_cache,
    decode_lengths,
    request_slot,
):
    rows = prefill_tokens.shape[0]
    exponent = jnp.arange(HALF, dtype=F32) * (2.0 / HEAD)
    frequency = (ROPE_BASE ** (-exponent))[:, None]
    positions = jnp.concatenate(
        [prefill_offsets[0].astype(F32) + jnp.arange(rows, dtype=F32), decode_lengths.astype(F32)]
    )
    angles = frequency * positions[None, :]
    cosine, sine = jnp.cos(angles), jnp.sin(angles)
    projected, dec = project(
        prefill_tokens, decode_tokens, attention_gain, qkv_weight.transpose(1, 2, 0), cosine, sine
    )
    hidden, dhidden = attention(
        n, projected, dec, cosine, sine, request_slot, prefill_offsets, decode_lengths,
        prefill_cache[0].transpose(0, 2, 1), decode_cache.transpose(0, 1, 3, 2), out_weight,
        prefill_tokens, decode_tokens,
    )
    hidden, dhidden, normed, dnormed = final_norm(feedforward_gain, hidden, dhidden)
    return hidden, dhidden, normed, dnormed


def solution(mesh):
    placed = (
        P("seq", None),
        P("seq", None),
        P(),
        P(None, None, "tp"),
        P("tp", None),
        P(),
        P("seq", None, None, "tp"),
        P("seq"),
        P("seq", None, None, "tp"),
        P("seq"),
        P(),
    )
    return jax.shard_map(
        functools.partial(local_step, mesh.shape["seq"]),
        mesh=mesh,
        in_specs=placed,
        out_specs=(P("seq", None), P("seq", None), P("seq", None), P("seq", None)),
        check_vma=False,
    )
```
